32 devices in a mesh: gx: 2 (over x), gy: 4 (over y, core), gz: 4 (over z).
Axes of the slice: x: 2, y: 2, z: 4, core: 2. Of those that a mesh axis runs over, the one named last changes fastest.
Arguments:
- states: float32 [19, 32, 64, 512], P(None, 'gx', 'gy', 'gz'), may hold values from 0 to 1
- active: int32 [4, 4, 4], P('gx', 'gy', 'gz'), may hold values 0 or 1
- fibre_index: int32 [4, 4, 4], P('gx', 'gy', 'gz'), may hold values from 0 to 63
- fibre_angle: float32 [2, 64], replicated, may hold values from -3.140625 to 3.140625
- conduct: float32 [2, 64], replicated, may hold values from 0.05 to 0.3
- gate_half: float32 [17], replicated, may hold values from 0.1 to 0.9
- gate_slope: float32 [17], replicated, may hold values from 0.05 to 0.3
- gate_tau: float32 [17], replicated, may hold values from 2 to 60
- conductance: float32 [17], replicated, may hold values from 0.005 to 0.05
- reversal: float32 [17], replicated, may hold values from -1 to 1.5
- block_elem: int32 [16, 32, 16], P('gx', 'gy', 'gz'), may hold values from 0 to 8191, as said below
- block_weight: float32 [16, 32, 16], P('gx', 'gy', 'gz'), may hold values from 0.5 to 1.5
- node_disp: float32 [3, 16384], P(None, ('gx', 'gy', 'gz')), may hold values from -0.15 to 0.15
- elem_node: int32 [8, 8192], P(None, ('gx', 'gy', 'gz')), may hold values from 0 to 404, as said below
- elem_fibre: int32 [8192], P(('gx', 'gy', 'gz')), may hold values from 0 to 63
- material: float32 [3], replicated, may hold values from 0.5 to 2
Outputs:
- new_states: float32 [19, 32, 64, 512], P(None, 'gx', 'gy', 'gz')
- fine_disp: float32 [3, 32, 64, 512], P(None, 'gx', 'gy', 'gz')
- node_residual: float32 [3, 16384], P(None, ('gx', 'gy', 'gz'))
The draws below stay inside these ranges and needn't reach their ends.
Inputs may be any that keep to these rules, and one draw needn't show every extreme that they name: `block_elem`: element numbers of the coarse partition: owner device e // 256, local element e % 256. Every element holds exactly one coupling block. Of the coupling blocks of one device at most 16 lie in elements of one owner device, and for every device some owner receives exactly 16 of them. `elem_node`: each column names eight distinct owner-local nodes of a hexahedral element of a structured partition, corner 4 i + 2 j + k at offset (i, j, k); neighbouring elements of one owner share nodes.
All inputs are finite; a program needn't handle non-finite values. No bound on the sum of `active` on one device may be relied on, other than what follows from the above.
Results may differ from the reference program's by a relative error of at most 0.0003.
Values sent between devices are 32-bit elements; how exact they have to be, the bound alone decides.
A program may use at most 64 MiB of HBM per device.

```python
import math
import jax
import jax.numpy as jnp
from jax import lax

NSTATE = 19
NCH = 17
NF = 64
TLX = 8
TLY = 16
TLZ = 128
SBX = 2
SBY = 2
SBZ = 32
FINE_STEPS = 2
ELX = 8
ELY = 8
CX = 16
CY = 16
CZ = 128
NX = 32
NY = 64
NZ = 512
TX = 4
TY = 4
TZ = 4
BX = 16
BY = 32
BZ = 16
ELZ = 4
ELEM_DEV = 256
NODE_DEV = 512
ELEMS = 8192
NODES = 16384


def draw_block_elem(key, part):
    grid_x = NX // CX
    grid_y = NY // CY
    grid_z = NZ // CZ
    device_count = grid_x * grid_y * grid_z
    blocks_x = CX // SBX
    blocks_y = CY // SBY
    blocks_z = CZ // SBZ
    block_count = blocks_x * blocks_y * blocks_z
    capacity = 2 * block_count // device_count
    halfcap = capacity // 2
    slot_count = device_count * capacity
    base = jax.random.fold_in(key, 7)
    first, second, third, fourth = jax.random.split(base, 4)
    shift_full = jax.random.randint(first, (), 0, device_count, dtype=jnp.int32)
    shift_empty = (shift_full + jax.random.randint(second, (), 1, device_count, dtype=jnp.int32)) % device_count
    sigma = jax.random.permutation(third, device_count).astype(jnp.int32)
    distance = (sigma[None, :] - sigma[:, None]) % device_count
    counts = halfcap + halfcap * (distance == shift_full).astype(jnp.int32) - halfcap * (distance == shift_empty).astype(jnp.int32)
    starts = jnp.cumsum(counts, axis=0) - counts

    def owner_perm(index):
        return jax.random.permutation(jax.random.fold_in(fourth, index), ELEM_DEV).astype(jnp.int32)
    perms = jax.vmap(owner_perm)(jnp.arange(device_count, dtype=jnp.int32))

    def one_device(index):
        inner = jax.random.fold_in(jax.random.fold_in(key, 13), index)
        owners = jnp.arange(device_count, dtype=jnp.int32)[:, None]
        ranks = jnp.arange(capacity, dtype=jnp.int32)[None, :]
        valid = ranks < counts[index][:, None]
        where = jnp.clip(starts[index][:, None] + ranks, 0, ELEM_DEV - 1)
        local = perms[owners, where]
        ids = (owners * ELEM_DEV + local).reshape(-1)
        places = jnp.arange(slot_count, dtype=jnp.int32)
        score = jnp.where(valid.reshape(-1), slot_count + places, places)
        unused, chosen = lax.top_k(score, block_count)
        order = jax.random.permutation(inner, block_count)
        return ids[chosen][order].reshape(blocks_x, blocks_y, blocks_z)
    every = jax.vmap(one_device)(jnp.arange(device_count, dtype=jnp.int32))
    every = every.reshape(grid_x, grid_y, grid_z, blocks_x, blocks_y, blocks_z)
    return every.transpose(0, 3, 1, 4, 2, 5).reshape(grid_x * blocks_x, grid_y * blocks_y, grid_z * blocks_z)


def draw_elem_node(key, part):
    device_count = ELEMS // ELEM_DEV
    used = (ELX + 1) * (ELY + 1) * (ELZ + 1)
    corner = jnp.arange(8, dtype=jnp.int32)[:, None]
    cell = jnp.arange(ELEM_DEV, dtype=jnp.int32)[None, :]
    node_x = cell // (ELY * ELZ) + corner // 4
    node_y = cell // ELZ % ELY + corner // 2 % 2
    node_z = cell % ELZ + corner % 2
    structured = (node_x * (ELY + 1) + node_y) * (ELZ + 1) + node_z

    def one_device(index):
        inner = jax.random.fold_in(jax.random.fold_in(key, 11), index)
        first, second = jax.random.split(inner)
        label = jax.random.permutation(first, used).astype(jnp.int32)
        order = jax.random.permutation(second, ELEM_DEV)
        return label[structured][:, order]
    every = jax.vmap(one_device)(jnp.arange(device_count, dtype=jnp.int32))
    return every.transpose(1, 0, 2).reshape(8, device_count * ELEM_DEV)


def place_ends(array, stream_key, low, top_value):
    longest = array.shape.index(max(array.shape))
    spots = []
    for shift in (0, 1):
        where = [jax.random.randint(jax.random.fold_in(stream_key, axis), (), 0, length) for axis, length in enumerate(array.shape)]
        where[longest] = (where[longest] + shift) % array.shape[longest]
        spots.append(tuple(where))
    return array.at[spots[0]].set(low).at[spots[1]].set(top_value)


def block_levels(stream_key, shape, cuts, low, largest):
    factor_of, own = 1.0, jax.random.fold_in(stream_key, 6)
    for dim, shards_of in cuts:
        draws = jnp.exp(jax.random.uniform(jax.random.fold_in(own, dim), (shards_of,), jnp.float32, low / len(cuts), largest / len(cuts)))
        factor_of = factor_of * jnp.repeat(draws, shape[dim] // shards_of).reshape([-1 if axis == dim else 1 for axis in range(len(shape))])
    return factor_of


def scatter_about(own_key, dims, deviation, bound, cuts=(), held_as=jnp.bfloat16):
    level = block_levels(own_key, dims, cuts, -0.22, 0.18) if cuts else 1.0
    drawn = jax.random.normal(own_key, dims, jnp.float32) * deviation * level
    return jnp.minimum(jnp.maximum(drawn, -bound), bound).astype(held_as)


def setup_inputs(seed: int = 0) -> dict:
    arg_keys = jax.random.split(jax.random.key(seed), 17)
    states = jnp.clip(1.0 * jax.random.uniform(arg_keys[0], (NSTATE, NX, NY, NZ), jnp.float32) ** block_levels(arg_keys[0], (NSTATE, NX, NY, NZ), ((1, 2), (2, 4), (3, 4)), -0.2, 0.2), 0.0, 1.0)
    active = place_ends((jax.random.randint(arg_keys[1], (TX, TY, TZ), 0, 4) < 3).astype(jnp.int32), jax.random.fold_in(arg_keys[1], 1), 0, 1)
    fibre_index = place_ends(jax.random.randint(arg_keys[2], (TX, TY, TZ), 0, NF), jax.random.fold_in(arg_keys[2], 1), 0, NF - 1).astype(jnp.int32)
    fibre_angle = jnp.clip(jax.random.uniform(arg_keys[3], (2, NF), jnp.float32, -3.140625, 3.140625), -3.140625, 3.140625)
    conduct = jnp.clip(jnp.exp(jax.random.uniform(arg_keys[4], (2, NF), jnp.float32, math.log(0.05), math.log(0.3))), 0.05, 0.3)
    gate_half = jnp.clip(jax.random.uniform(arg_keys[5], (NCH,), jnp.float32, 0.1, 0.9), 0.1, 0.9)
    gate_slope = jnp.clip(jnp.exp(jax.random.uniform(arg_keys[6], (NCH,), jnp.float32, math.log(0.05), math.log(0.3))), 0.05, 0.3)
    gate_tau = jnp.clip(jnp.exp(jax.random.uniform(arg_keys[7], (NCH,), jnp.float32, math.log(2.0), math.log(60.0))), 2.0, 60.0)
    conductance = jnp.clip(jnp.exp(jax.random.uniform(arg_keys[8], (NCH,), jnp.float32, math.log(0.005), math.log(0.05))), 0.005, 0.05)
    reversal = jnp.clip(jax.random.uniform(arg_keys[9], (NCH,), jnp.float32, -1.0, 1.5), -1.0, 1.5)
    block_elem = draw_block_elem(jax.random.fold_in(arg_keys[16], 71), 0)
    block_weight = jnp.clip(0.5 + 1.0 * jax.random.uniform(arg_keys[11], (BX, BY, BZ), jnp.float32) ** block_levels(arg_keys[11], (BX, BY, BZ), ((0, 2), (1, 4), (2, 4)), -0.2, 0.2), 0.5, 1.5)
    node_disp = scatter_about(arg_keys[12], (3, NODES), 0.05, 0.15, ((1, 32),), jnp.float32)
    elem_node = draw_elem_node(jax.random.fold_in(arg_keys[16], 71), 0)
    elem_fibre = place_ends(jax.random.randint(arg_keys[14], (ELEMS,), 0, NF), jax.random.fold_in(arg_keys[14], 1), 0, NF - 1).astype(jnp.int32)
    material = jnp.clip(jnp.exp(jax.random.uniform(arg_keys[15], (3,), jnp.float32, math.log(0.5), math.log(2.0))), 0.5, 2.0)
    return {"states": states, "active": active, "fibre_index": fibre_index, "fibre_angle": fibre_angle, "conduct": conduct, "gate_half": gate_half, "gate_slope": gate_slope, "gate_tau": gate_tau, "conductance": conductance, "reversal": reversal, "block_elem": block_elem, "block_weight": block_weight, "node_disp": node_disp, "elem_node": elem_node, "elem_fibre": elem_fibre, "material": material}


calcium_keep = 0.9
tension_half = 0.09
highest = lax.Precision.HIGHEST


def fibre_frame(first_angle, second_angle):
    return jnp.stack([jnp.cos(first_angle) * jnp.cos(second_angle), jnp.sin(first_angle) * jnp.cos(second_angle), jnp.sin(second_angle)], 0)


def coefficients(frame, along, across, live_tile):
    spread = along - across
    return jnp.stack([across + spread * frame[0] * frame[0], across + spread * frame[1] * frame[1], across + spread * frame[2] * frame[2], spread * frame[0] * frame[1], spread * frame[0] * frame[2], spread * frame[1] * frame[2]], 0) * live_tile


def expand(tiles):
    return jnp.repeat(jnp.repeat(jnp.repeat(tiles, TLX, 1), TLY, 2), TLZ, 3)


def ionic(states, live, gate_half, gate_slope, gate_tau, conductance, reversal):
    volt = states[0]
    shape = (gate_half.shape[0],) + (1,) * (states.ndim - 1)
    steady = jax.nn.sigmoid((volt[None] - gate_half.reshape(shape)) / gate_slope.reshape(shape))
    keeping = jnp.exp(-1.0 / gate_tau).reshape(shape)
    old_gates = states[1:NSTATE - 1]
    gates = steady + (old_gates - steady) * keeping
    current = jnp.sum(conductance.reshape(shape) * gates * (volt[None] - reversal.reshape(shape)), axis=0)
    vstar = volt - current
    calcium = states[NSTATE - 1] * calcium_keep + (1.0 - calcium_keep) * jax.nn.sigmoid(8.0 * (volt - 0.5))
    alive = live > 0.5
    gates = jnp.where(alive[None], gates, old_gates)
    vstar = jnp.where(alive, vstar, volt)
    calcium = jnp.where(alive, calcium, states[NSTATE - 1])
    return gates, vstar, calcium


def fluxes(padded, coef):
    grad_x = (padded[2:, 1:-1, 1:-1] - padded[:-2, 1:-1, 1:-1]) * 0.5
    grad_y = (padded[1:-1, 2:, 1:-1] - padded[1:-1, :-2, 1:-1]) * 0.5
    grad_z = (padded[1:-1, 1:-1, 2:] - padded[1:-1, 1:-1, :-2]) * 0.5
    return jnp.stack([coef[0] * grad_x + coef[3] * grad_y + coef[4] * grad_z, coef[3] * grad_x + coef[1] * grad_y + coef[5] * grad_z, coef[4] * grad_x + coef[5] * grad_y + coef[2] * grad_z], 0)


def divergence(flux):
    return (flux[0, 2:, 1:-1, 1:-1] - flux[0, :-2, 1:-1, 1:-1]) * 0.5 + (flux[1, 1:-1, 2:, 1:-1] - flux[1, 1:-1, :-2, 1:-1]) * 0.5 + (flux[2, 1:-1, 1:-1, 2:] - flux[2, 1:-1, 1:-1, :-2]) * 0.5


def corner_bits():
    corner = jnp.arange(8, dtype=jnp.int32)
    return jnp.stack([corner // 4, (corner // 2) % 2, corner % 2], 1).astype(jnp.float32)


def shape_gradients():
    return (2.0 * corner_bits() - 1.0) * 0.25


def blend_weights():
    bits = corner_bits()
    place = jnp.arange(SBX * SBY * SBZ, dtype=jnp.int32)
    along_x = ((place // (SBY * SBZ)).astype(jnp.float32) + 0.5) / SBX
    along_y = (((place // SBZ) % SBY).astype(jnp.float32) + 0.5) / SBY
    along_z = ((place % SBZ).astype(jnp.float32) + 0.5) / SBZ
    local = jnp.stack([along_x, along_y, along_z], 0)
    factor = jnp.where(bits[:, :, None] > 0.5, local[None], 1.0 - local[None])
    return factor[:, 0] * factor[:, 1] * factor[:, 2]


def element_forces(corner_disp, frame, tension, material):
    grads = shape_gradients()
    deform = jnp.einsum('iae,aj->ije', corner_disp, grads, precision=highest) + jnp.eye(3, dtype=jnp.float32)[:, :, None]
    cof = jnp.stack([
        jnp.stack([deform[1, 1] * deform[2, 2] - deform[1, 2] * deform[2, 1], deform[1, 2] * deform[2, 0] - deform[1, 0] * deform[2, 2], deform[1, 0] * deform[2, 1] - deform[1, 1] * deform[2, 0]], 0),
        jnp.stack([deform[0, 2] * deform[2, 1] - deform[0, 1] * deform[2, 2], deform[0, 0] * deform[2, 2] - deform[0, 2] * deform[2, 0], deform[0, 1] * deform[2, 0] - deform[0, 0] * deform[2, 1]], 0),
        jnp.stack([deform[0, 1] * deform[1, 2] - deform[0, 2] * deform[1, 1], deform[0, 2] * deform[1, 0] - deform[0, 0] * deform[1, 2], deform[0, 0] * deform[1, 1] - deform[0, 1] * deform[1, 0]], 0)], 0)
    volume = deform[0, 0] * cof[0, 0] + deform[0, 1] * cof[0, 1] + deform[0, 2] * cof[0, 2]
    inverse_t = cof / volume
    stretch = jnp.sum(deform * frame[None], axis=1)
    stress = material[0] * (deform - inverse_t) + material[1] * jnp.log(volume) * inverse_t + material[2] * tension * stretch[:, None] * frame[None]
    return jnp.einsum('ije,aj->iae', stress, grads, precision=highest)


def reference(states, active, fibre_index, fibre_angle, conduct, gate_half, gate_slope, gate_tau, conductance, reversal, block_elem, block_weight, node_disp, elem_node, elem_fibre, material):
    frame = fibre_frame(fibre_angle[0][fibre_index], fibre_angle[1][fibre_index])
    live_tile = (active > 0).astype(jnp.float32)
    coef = expand(coefficients(frame, conduct[0][fibre_index], conduct[1][fibre_index], live_tile))
    live = expand(live_tile[None])[0]
    for step in range(FINE_STEPS):
        gates, vstar, calcium = ionic(states, live, gate_half, gate_slope, gate_tau, conductance, reversal)
        flux = fluxes(jnp.pad(vstar, 1), coef)
        lap = divergence(jnp.pad(flux, ((0, 0), (1, 1), (1, 1), (1, 1))))
        states = jnp.concatenate([(vstar + live * lap)[None], gates, calcium[None]], 0)
    calcium = states[NSTATE - 1]
    tension = calcium * calcium / (calcium * calcium + tension_half)
    block_mean = tension.reshape(BX, SBX, BY, SBY, BZ, SBZ).mean(axis=(1, 3, 5)).reshape(-1)
    block_value = block_weight.reshape(-1) * block_mean
    flat_ids = block_elem.reshape(-1)
    elem_tension = jax.ops.segment_sum(block_value, flat_ids, num_segments=ELEMS)
    owner = jnp.arange(ELEMS, dtype=jnp.int32) // ELEM_DEV
    global_nodes = owner[None, :] * NODE_DEV + elem_node
    corner_disp = node_disp[:, global_nodes]
    elem_frame = fibre_frame(fibre_angle[0][elem_fibre], fibre_angle[1][elem_fibre])
    force = element_forces(corner_disp, elem_frame, elem_tension, material)
    flat_nodes = global_nodes.reshape(-1)
    node_residual = jnp.stack([jax.ops.segment_sum(force[k].reshape(-1), flat_nodes, num_segments=NODES) for k in range(3)], 0)
    block_nodes = (flat_ids // ELEM_DEV)[None, :] * NODE_DEV + elem_node[:, flat_ids]
    block_disp = node_disp[:, block_nodes]
    fine = jnp.einsum('cab,ap->cbp', block_disp, blend_weights(), precision=highest)
    fine_disp = fine.reshape(3, BX, BY, BZ, SBX, SBY, SBZ).transpose(0, 1, 4, 2, 5, 3, 6).reshape(3, NX, NY, NZ)
    return states, fine_disp, node_residual
```

```python
import functools

import jax
import jax.numpy as jnp
from jax import lax
from jax.experimental import pallas as pl
from jax.experimental.pallas import tpu as pltpu
from jax.sharding import PartitionSpec as P

NSTATE = 19
TLX = 8
SBX = 2
SBY = 2
SBZ = 32
FINE_STEPS = 2
AXES = ("gx", "gy", "gz")
MESH = pl.DeviceIdType.MESH
LANES = 128
f32 = jnp.float32
bf16 = jnp.bfloat16
calcium_keep = 0.9
tension_half = 0.09
NN = (((1,), (0,)), ((), ()))
NT = (((1,), (1,)), ((), ()))


def mm(a, b, dims=NN):
    return lax.dot_general(a, b, dims, preferred_element_type=f32)


def parts3(x):
    x1 = x.astype(bf16)
    r1 = x - x1.astype(f32)
    x2 = r1.astype(bf16)
    x3 = (r1 - x2.astype(f32)).astype(bf16)
    return x1, x2, x3


def rows3(x):
    return jnp.concatenate([p.astype(f32) for p in parts3(x)], 0).astype(bf16)


def fold3(y):
    r = y.shape[0] // 3
    return y[:r] + y[r : 2 * r] + y[2 * r :]


def mm_right3(a, x, dims=NN):
    x1, x2, x3 = parts3(x)
    return mm(a, x1, dims) + mm(a, x2, dims) + mm(a, x3, dims)


def iota(shape, dim):
    return lax.broadcasted_iota(jnp.int32, shape, dim)


def column(row):
    pieces = [
        jnp.transpose(jnp.broadcast_to(row[:, i : i + LANES], (LANES, LANES)))
        for i in range(0, row.shape[1], LANES)
    ]
    return pieces[0] if len(pieces) == 1 else jnp.concatenate(pieces, 0)


def onehot(mask):
    return jnp.where(mask, 1.0, 0.0).astype(bf16)


def pick_rows(rows, shape):
    index = iota(shape, 0)
    out = jnp.zeros(shape, f32)
    for i, row in enumerate(rows):
        out = jnp.where(index == i, row, out)
    return out


def sigmoid(u):
    return 0.5 * jnp.tanh(0.5 * u) + 0.5


def frame_of(a, b):
    return jnp.cos(a) * jnp.cos(b), jnp.sin(a) * jnp.cos(b), jnp.sin(b)


def body(
    sizes,
    states,
    active,
    fibre_index,
    angle_s,
    angle_v,
    conduct,
    gate_half,
    gate_slope,
    gate_tau,
    conductance,
    reversal,
    ids_ref,
    weight_ref,
    node_disp,
    elem_node,
    elem_fibre,
    material,
    out,
    fine_out,
    resid_out,
    vs,
    flux,
    send_y,
    send_z,
    halo_x,
    halo_y,
    halo_z,
    corner_oh,
    corner_cd,
    slot_oh,
    pick_oh,
    owner_oh,
    rank_oh,
    ids_send,
    ids_got,
    val_send,
    val_got,
    ans_send,
    ans_got,
    face_send_sem,
    face_recv_sem,
    all_send_sem,
    all_recv_sem,
):
    mx, my, mz, seats, elem_count = sizes
    n = mx * my * mz
    nx, ny, nz = states.shape[1:]
    gates_n = NSTATE - 2
    bx, by, bz = nx // SBX, ny // SBY, nz // SBZ
    plane = bx * by
    blocks = plane * bz
    slots = n * seats
    tiles = nx // TLX
    node_count = node_disp.shape[1]
    corners = 8
    cx, cy, cz = (lax.axis_index(a) for a in AXES)
    me = (cx * my + cy) * mz + cz

    def coords(flat):
        return flat // (my * mz), (flat // mz) % my, flat % mz

    barrier = pltpu.get_barrier_semaphore()

    def greet(k, carry):
        pl.semaphore_signal(
            barrier, inc=1, device_id=coords((me + k) % n), device_id_type=MESH
        )
        return carry

    lax.fori_loop(1, n, greet, 0)

    def splat(value):
        return jnp.full((1, 1, LANES), value, f32)

    coef, live = [], []
    for t in range(tiles):
        index = fibre_index[t, 0, 0]
        fx, fy, fz = frame_of(splat(angle_s[0, index]), splat(angle_s[1, index]))
        across = splat(conduct[1, index])
        spread = splat(conduct[0, index]) - across
        alive = splat(jnp.where(active[t, 0, 0] > 0, 1.0, 0.0).astype(f32))
        live.append(alive)
        coef.append(
            [
                (across + spread * fx * fx) * alive,
                (across + spread * fy * fy) * alive,
                (across + spread * fz * fz) * alive,
                spread * fx * fy * alive,
                spread * fx * fz * alive,
                spread * fy * fz * alive,
            ]
        )

    chunk = 4

    def ionic(source, t):
        alive = live[t] > 0.5

        def step(i, carry):
            at = pl.ds(t * TLX + i * chunk, chunk)
            volt = source[0, at]
            current = jnp.zeros_like(volt)
            for g in range(gates_n):
                inv = 1.0 / splat(gate_slope[g])
                keep = jnp.exp(-1.0 / splat(gate_tau[g]))
                steady = sigmoid((volt - splat(gate_half[g])) * inv)
                old = source[1 + g, at]
                gate = steady + (old - steady) * keep
                current = current + splat(conductance[g]) * gate * (volt - splat(reversal[g]))
                out[1 + g, at] = jnp.where(alive, gate, old)
            old = source[NSTATE - 1, at]
            calcium = old * calcium_keep + (1.0 - calcium_keep) * sigmoid(8.0 * (volt - 0.5))
            out[NSTATE - 1, at] = jnp.where(alive, calcium, old)
            vs[at] = jnp.where(alive, volt - current, volt)
            return carry

        lax.fori_loop(0, TLX // chunk, step, 0)

    def face_copies(stage, low_x, high_x):
        near = [(cx, mx), (cy, my), (cz, mz)]
        made = []
        for dim in range(3):
            for side in range(2):
                if dim == 0:
                    src = high_x if side == 0 else low_x
                    dst = halo_x.at[stage, side]
                elif dim == 1:
                    src, dst = send_y.at[stage, side], halo_y.at[stage, side]
                else:
                    src, dst = send_z.at[stage, side], halo_z.at[stage, side]
                at, count = near[dim]
                to = [cx, cy, cz]
                to[dim] = (at + (1 if side == 0 else count - 1)) % count
                made.append(
                    pltpu.make_async_remote_copy(
                        src_ref=src,
                        dst_ref=dst,
                        send_sem=face_send_sem.at[stage, 2 * dim + side],
                        recv_sem=face_recv_sem.at[stage, 2 * dim + side],
                        device_id=tuple(to),
                        device_id_type=MESH,
                    )
                )
        return made

    def flat_z(a):
        return jnp.transpose(a.reshape(nx * ny, nz))

    def send_faces(stage, a_y, a_z, low_x, high_x):
        send_y[stage, 0] = a_y[:, ny - 1 : ny, :]
        send_y[stage, 1] = a_y[:, 0:1, :]
        turned = flat_z(a_z)
        send_z[stage, 0] = turned[nz - 1 : nz, :]
        send_z[stage, 1] = turned[0:1, :]
        copies = face_copies(stage, low_x, high_x)
        for c in copies:
            c.start()
        return copies

    def masked(value, inside):
        return jnp.where(inside, value, 0.0)

    def diff_x(a, stage):
        low = masked(halo_x[stage, 0], cx > 0)[None]
        high = masked(halo_x[stage, 1], cx < mx - 1)[None]
        up = jnp.concatenate([a[1:], high], 0)
        down = jnp.concatenate([low, a[:-1]], 0)
        return (up - down) * 0.5

    def diff_y(a, stage):
        low = masked(halo_y[stage, 0], cy > 0)
        high = masked(halo_y[stage, 1], cy < my - 1)
        row = iota((1, ny, nz), 1)
        down = jnp.where(row == 0, low, pltpu.roll(a, 1, 1))
        up = jnp.where(row == ny - 1, high, pltpu.roll(a, ny - 1, 1))
        return (up - down) * 0.5

    def diff_z(a, stage):
        low = masked(halo_z[stage, 0], cz > 0)
        high = masked(halo_z[stage, 1], cz < mz - 1)
        row = iota((nz, nx * ny), 0)
        edge = jnp.where(row == 0, low, jnp.where(row == nz - 1, high, 0.0))
        edge = jnp.transpose(edge).reshape(nx, ny, nz)
        lane = iota((1, 1, nz), 2)
        down = jnp.where(lane == 0, edge, pltpu.roll(a, 1, 2))
        up = jnp.where(lane == nz - 1, edge, pltpu.roll(a, nz - 1, 2))
        return (up - down) * 0.5

    def make_flux(stage):
        v = vs[...]
        gx, gy, gz = diff_x(v, stage), diff_y(v, stage), diff_z(v, stage)
        for t in range(tiles):
            at = slice(t * TLX, (t + 1) * TLX)
            xx, yy, zz, xy, xz, yz = coef[t]
            a, b, c = gx[at], gy[at], gz[at]
            flux[0, at] = xx * a + xy * b + xz * c
            flux[1, at] = xy * a + yy * b + yz * c
            flux[2, at] = xz * a + yz * b + zz * c

    def finish(stage):
        lap = diff_x(flux[0], stage) + diff_y(flux[1], stage) + diff_z(flux[2], stage)
        for t in range(tiles):
            at = slice(t * TLX, (t + 1) * TLX)
            out[0, at] = vs[at] + live[t] * lap[at]

    def all_copy(k, kind, src, dst):
        return pltpu.make_async_remote_copy(
            src_ref=src.at[(me + k) % n],
            dst_ref=dst.at[me],
            send_sem=all_send_sem.at[kind, k],
            recv_sem=all_recv_sem.at[kind, k],
            device_id=coords((me + k) % n),
            device_id_type=MESH,
        )

    def all_start(kind, src, dst):
        dst[pl.ds(me, 1)] = src[pl.ds(me, 1)]

        def go(k, carry):
            all_copy(k, kind, src, dst).start()
            return carry

        lax.fori_loop(1, n, go, 0)

    def all_wait(kind, src, dst):
        def go(k, carry):
            pltpu.make_async_remote_copy(
                src_ref=src.at[(me + k) % n],
                dst_ref=dst.at[(me + n - k) % n],
                send_sem=all_send_sem.at[kind, k],
                recv_sem=all_recv_sem.at[kind, k],
                device_id=coords((me + k) % n),
                device_id_type=MESH,
            ).wait()
            return carry

        lax.fori_loop(1, n, go, 0)

    per_row = LANES // seats
    groups = slots // LANES

    def lanes_of(got):
        pieces = []
        for g in range(groups):
            pieces.append(
                lax.fori_loop(
                    0,
                    per_row,
                    lambda r, acc, g=g: acc + got[g * per_row + r],
                    jnp.zeros((1, LANES), f32),
                )
            )
        return jnp.concatenate(pieces, 1)

    for t in range(tiles):
        ionic(states, t)
    shift = elem_count.bit_length() - 1
    ids = ids_ref[...]
    owner = lax.shift_right_logical(ids, shift)
    local = ids - owner * elem_count
    owner_col = column(owner.astype(f32))
    owner_f = owner.astype(f32)
    owner_cols = jnp.concatenate([owner_col] * (blocks // LANES), 1)
    earlier = (owner_cols == owner_f) & (iota((blocks, blocks), 1) < iota((blocks, blocks), 0))
    rank = jnp.sum(jnp.where(earlier, 1.0, 0.0), axis=1, keepdims=True)
    offset = ((me % per_row) * seats).astype(f32)
    rank_hit = onehot(iota((blocks, LANES), 1).astype(f32) == rank + offset)
    rank_oh[...] = rank_hit
    owned = owner == iota((n, blocks), 0)
    owner_oh[...] = onehot(owned)
    slot_col = owner_col[:, 0:1] * seats + rank
    slot_oh[...] = onehot(iota((blocks, slots), 1).astype(f32) == slot_col)
    wanted = jnp.where(owned, local.astype(f32) + 1.0, 0.0).astype(bf16)
    ids_send[...] = mm(wanted, rank_hit).reshape(n, 1, LANES)

    pl.semaphore_wait(barrier, n - 1)
    v0 = vs[...]
    stage0 = send_faces(0, v0, v0, vs.at[0], vs.at[nx - 1])
    all_start(0, ids_send, ids_got)

    nodes = pick_rows([node_disp[i : i + 1, :] for i in range(3)], (8, node_count))
    nodes3 = rows3(nodes)
    for q in range(corners):
        hit = onehot(iota((node_count, elem_count), 0) == elem_node[q : q + 1, :])
        corner_oh[q] = hit
        corner_cd[q] = fold3(mm(nodes3, hit))

    for c in stage0:
        c.wait()
    make_flux(0)
    stage1 = send_faces(1, flux[1], flux[2], flux.at[0, 0], flux.at[0, nx - 1])

    all_wait(0, ids_send, ids_got)
    asked = column(lanes_of(ids_got)) - 1.0
    asked = jnp.concatenate([asked] * (elem_count // LANES), 1)
    pick_oh[...] = onehot(iota((slots, elem_count), 1).astype(f32) == asked)
    table = jnp.concatenate(
        [corner_cd[...].reshape(corners * 8, elem_count), jnp.zeros((LANES - corners * 8, elem_count), f32)],
        0,
    )
    ans_send[...] = mm_right3(pick_oh[...], table, NT).reshape(n, seats, LANES)
    all_start(1, ans_send, ans_got)

    for c in stage1:
        c.wait()
    finish(1)
    for t in range(tiles):
        ionic(out, t)
    v1 = vs[...]
    stage2 = send_faces(2, v1, v1, vs.at[0], vs.at[nx - 1])

    calcium = out[NSTATE - 1]
    square = calcium * calcium
    pull = (square / (square + tension_half)).reshape(bx, SBX, ny, nz)
    pull = (pull[:, 0] + pull[:, 1]).reshape(bx * ny, nz)
    pair = onehot(iota((plane, bx * ny), 1) // SBY == iota((plane, bx * ny), 0))
    pooled = mm_right3(pair, pull)
    strip = onehot(iota((nz, LANES), 0) // SBZ == iota((nz, LANES), 1))
    pooled = fold3(mm(rows3(pooled), strip)) * (1.0 / (SBX * SBY * SBZ))
    worth = jnp.concatenate(
        [
            jnp.broadcast_to(pooled[:, b : b + 1] * weight_ref[:, b : b + 1], (plane, LANES))
            for b in range(bz)
        ],
        0,
    )
    worth = jnp.where(rank_oh[...].astype(f32) > 0.5, worth, 0.0)
    val_send[...] = mm_right3(owner_oh[...], worth).reshape(n, 1, LANES)
    all_start(2, val_send, val_got)

    angle = angle_v[...]
    fx, fy, fz = frame_of(angle[0:1, :], angle[1:2, :])
    entries = angle.shape[1]
    fibres = pick_rows([fx, fy, fz], (8, entries))
    which = onehot(iota((entries, elem_count), 0) == elem_fibre[...])
    frames = fold3(mm(rows3(fibres), which))
    frame = [frames[i : i + 1, :] for i in range(3)]
    grads = [
        [((2 * (q // 4) - 1) / 4), ((2 * (q // 2 % 2) - 1) / 4), ((2 * (q % 2) - 1) / 4)]
        for q in range(corners)
    ]
    sums = [sum(corner_cd[q] * grads[q][j] for q in range(corners)) for j in range(3)]
    d = [
        [sums[j][i : i + 1, :] + (1.0 if i == j else 0.0) for j in range(3)] for i in range(3)
    ]
    cof = [
        [
            d[(i + 1) % 3][(j + 1) % 3] * d[(i + 2) % 3][(j + 2) % 3]
            - d[(i + 1) % 3][(j + 2) % 3] * d[(i + 2) % 3][(j + 1) % 3]
            for j in range(3)
        ]
        for i in range(3)
    ]
    volume = d[0][0] * cof[0][0] + d[0][1] * cof[0][1] + d[0][2] * cof[0][2]
    inverse = 1.0 / volume
    logv = jnp.log(volume)
    shear, bulk, scale = material[0], material[1], material[2]
    passive = [
        [
            shear * (d[i][j] - cof[i][j] * inverse) + bulk * logv * (cof[i][j] * inverse)
            for j in range(3)
        ]
        for i in range(3)
    ]
    stretch = [
        scale * (d[i][0] * frame[0] + d[i][1] * frame[1] + d[i][2] * frame[2]) for i in range(3)
    ]

    for c in stage2:
        c.wait()
    make_flux(2)
    stage3 = send_faces(3, flux[1], flux[2], flux.at[0, 0], flux.at[0, nx - 1])

    all_wait(1, ans_send, ans_got)
    returned = ans_got[...].reshape(slots, LANES)
    near = mm_right3(slot_oh[...], returned)
    lane = iota((plane, nz), 1)
    strip_of = lane // SBZ
    xi = ((lane % SBZ).astype(f32) + 0.5) / SBZ
    for c in range(3):
        lines = []
        for ij in range(4):
            ends = []
            for k in range(2):
                col = (2 * ij + k) * 8 + c
                value = jnp.zeros((plane, nz), f32)
                for b in range(bz):
                    value = jnp.where(
                        strip_of == b, near[b * plane : (b + 1) * plane, col : col + 1], value
                    )
                ends.append(value)
            lines.append(ends[0] * (1.0 - xi) + ends[1] * xi)
        for iv in range(SBX):
            wx = (iv + 0.5) / SBX
            for jv in range(SBY):
                wy = (jv + 0.5) / SBY
                value = (
                    lines[0] * ((1 - wx) * (1 - wy))
                    + lines[1] * ((1 - wx) * wy)
                    + lines[2] * (wx * (1 - wy))
                    + lines[3] * (wx * wy)
                )
                for p in range(bx):
                    fine_out[c, SBX * p + iv, pl.ds(jv, by, stride=SBY), :] = value[
                        p * by : (p + 1) * by
                    ]

    for c in stage3:
        c.wait()
    finish(3)

    all_wait(2, val_send, val_got)
    arrived = jnp.broadcast_to(lanes_of(val_got), (8, slots))
    tension = fold3(mm(rows3(arrived), pick_oh[...]))[0:1, :]
    total = jnp.zeros((24, node_count), f32)
    stress = [
        [passive[i][j] + tension * stretch[i] * frame[j] for j in range(3)] for i in range(3)
    ]
    for q in range(corners):
        force = pick_rows(
            [
                stress[i][0] * grads[q][0] + stress[i][1] * grads[q][1] + stress[i][2] * grads[q][2]
                for i in range(3)
            ],
            (8, elem_count),
        )
        total = total + mm(rows3(force), corner_oh[q], NT)
    resid_out[...] = fold3(total)[0:3, :]


def shards(
    states,
    active,
    fibre_index,
    fibre_angle,
    conduct,
    gate_half,
    gate_slope,
    gate_tau,
    conductance,
    reversal,
    block_elem,
    block_weight,
    node_disp,
    elem_node,
    elem_fibre,
    material,
):
    mx, my, mz = (lax.axis_size(a) for a in AXES)
    n = mx * my * mz
    elem_count = elem_node.shape[1]
    node_count = node_disp.shape[1]
    nx, ny, nz = states.shape[1:]
    bx, by, bz = block_elem.shape
    blocks = bx * by * bz
    seats = max(2 * blocks // n, 8)
    slots = n * seats
    ids = block_elem.transpose(2, 0, 1).reshape(1, blocks)
    weight = block_weight.reshape(bx * by, bz)
    vmem = pl.BlockSpec(memory_space=pltpu.VMEM)
    smem = pl.BlockSpec(memory_space=pltpu.SMEM)
    stages = 2 * FINE_STEPS
    return pl.pallas_call(
        functools.partial(body, (mx, my, mz, seats, elem_count)),
        out_shape=(
            jax.ShapeDtypeStruct(states.shape, f32),
            jax.ShapeDtypeStruct((3, nx, ny, nz), f32),
            jax.ShapeDtypeStruct((3, node_count), f32),
        ),
        in_specs=[vmem, smem, smem, smem, vmem] + [smem] * 6 + [vmem] * 5 + [smem],
        out_specs=(vmem, vmem, vmem),
        scratch_shapes=[
            pltpu.VMEM((nx, ny, nz), f32),
            pltpu.VMEM((3, nx, ny, nz), f32),
            pltpu.VMEM((stages, 2, nx, 1, nz), f32),
            pltpu.VMEM((stages, 2, 1, nx * ny), f32),
            pltpu.VMEM((stages, 2, ny, nz), f32),
            pltpu.VMEM((stages, 2, nx, 1, nz), f32),
            pltpu.VMEM((stages, 2, 1, nx * ny), f32),
            pltpu.VMEM((8, node_count, elem_count), bf16),
            pltpu.VMEM((8, 8, elem_count), f32),
            pltpu.VMEM((blocks, slots), bf16),
            pltpu.VMEM((slots, elem_count), bf16),
            pltpu.VMEM((n, blocks), bf16),
            pltpu.VMEM((blocks, LANES), bf16),
            pltpu.VMEM((n, 1, LANES), f32),
            pltpu.VMEM((n, 1, LANES), f32),
            pltpu.VMEM((n, 1, LANES), f32),
            pltpu.VMEM((n, 1, LANES), f32),
            pltpu.VMEM((n, seats, LANES), f32),
            pltpu.VMEM((n, seats, LANES), f32),
            pltpu.SemaphoreType.DMA((stages, 6)),
            pltpu.SemaphoreType.DMA((stages, 6)),
            pltpu.SemaphoreType.DMA((3, n)),
            pltpu.SemaphoreType.DMA((3, n)),
        ],
        compiler_params=pltpu.CompilerParams(
            collective_id=0, has_side_effects=True, vmem_limit_bytes=60 * 1024 * 1024
        ),
        name="step",
    )(
        states,
        active,
        fibre_index,
        fibre_angle,
        fibre_angle,
        conduct,
        gate_half,
        gate_slope,
        gate_tau,
        conductance,
        reversal,
        ids,
        weight,
        node_disp,
        elem_node,
        elem_fibre.reshape(1, elem_count),
        material,
    )


def solution(mesh):
    in_specs = (
        P(None, "gx", "gy", "gz"),
        P("gx", "gy", "gz"),
        P("gx", "gy", "gz"),
        P(),
        P(),
        P(),
        P(),
        P(),
        P(),
        P(),
        P("gx", "gy", "gz"),
        P("gx", "gy", "gz"),
        P(None, ("gx", "gy", "gz")),
        P(None, ("gx", "gy", "gz")),
        P(("gx", "gy", "gz")),
        P(),
    )
    out_specs = (P(None, "gx", "gy", "gz"), P(None, "gx", "gy", "gz"), P(None, ("gx", "gy", "gz")))
    return jax.shard_map(shards, mesh=mesh, in_specs=in_specs, out_specs=out_specs, check_vma=False)
```

```python
import functools

import jax
import jax.numpy as jnp
from jax import lax
from jax.experimental import pallas as pl
from jax.experimental.pallas import tpu as pltpu
from jax.sharding import PartitionSpec as P

NSTATE = 19
TLX = 8
SBX = 2
SBY = 2
SBZ = 32
FINE_STEPS = 2
AXES = ("gx", "gy", "gz")
MESH = pl.DeviceIdType.MESH
LANES = 128
f32 = jnp.float32
bf16 = jnp.bfloat16
calcium_keep = 0.9
tension_half = 0.09
NN = (((1,), (0,)), ((), ()))
NT = (((1,), (1,)), ((), ()))


def mm(a, b, dims=NN):
    return lax.dot_general(a, b, dims, preferred_element_type=f32)


def parts3(x):
    x1 = x.astype(bf16)
    r1 = x - x1.astype(f32)
    x2 = r1.astype(bf16)
    x3 = (r1 - x2.astype(f32)).astype(bf16)
    return x1, x2, x3


def rows3(x):
    return jnp.concatenate([p.astype(f32) for p in parts3(x)], 0).astype(bf16)


def fold3(y):
    r = y.shape[0] // 3
    return y[:r] + y[r : 2 * r] + y[2 * r :]


def mm_right3(a, x, dims=NN):
    x1, x2, x3 = parts3(x)
    return mm(a, x1, dims) + mm(a, x2, dims) + mm(a, x3, dims)


def iota(shape, dim):
    return lax.broadcasted_iota(jnp.int32, shape, dim)


def column(row):
    pieces = [
        jnp.transpose(jnp.broadcast_to(row[:, i : i + LANES], (LANES, LANES)))
        for i in range(0, row.shape[1], LANES)
    ]
    return pieces[0] if len(pieces) == 1 else jnp.concatenate(pieces, 0)


def onehot(mask):
    return jnp.where(mask, 1.0, 0.0).astype(bf16)


def pick_rows(rows, shape):
    index = iota(shape, 0)
    out = jnp.zeros(shape, f32)
    for i, row in enumerate(rows):
        out = jnp.where(index == i, row, out)
    return out


def sigmoid(u):
    return 0.5 * jnp.tanh(0.5 * u) + 0.5


def frame_of(a, b):
    return jnp.cos(a) * jnp.cos(b), jnp.sin(a) * jnp.cos(b), jnp.sin(b)


def body(
    sizes,
    states,
    active,
    fibre_index,
    angle_s,
    angle_v,
    conduct,
    gate_half,
    gate_slope,
    gate_tau,
    conductance,
    reversal,
    ids_ref,
    weight_ref,
    node_disp,
    elem_node,
    elem_fibre,
    material,
    out,
    fine_out,
    resid_out,
    vs,
    flux,
    send_y,
    send_z,
    halo_x,
    halo_y,
    halo_z,
    corner_oh,
    corner_cd,
    slot_oh,
    pick_oh,
    owner_oh,
    rank_oh,
    ids_send,
    ids_got,
    val_send,
    val_got,
    ans_send,
    ans_got,
    face_send_sem,
    face_recv_sem,
    all_send_sem,
    all_recv_sem,
):
    mx, my, mz, seats, elem_count = sizes
    n = mx * my * mz
    nx, ny, nz = states.shape[1:]
    gates_n = NSTATE - 2
    bx, by, bz = nx // SBX, ny // SBY, nz // SBZ
    plane = bx * by
    blocks = plane * bz
    slots = n * seats
    tiles = nx // TLX
    node_count = node_disp.shape[1]
    corners = 8
    cx, cy, cz = (lax.axis_index(a) for a in AXES)
    me = (cx * my + cy) * mz + cz

    def coords(flat):
        return flat // (my * mz), (flat // mz) % my, flat % mz

    barrier = pltpu.get_barrier_semaphore()

    def greet(k, carry):
        pl.semaphore_signal(
            barrier, inc=1, device_id=coords((me + k) % n), device_id_type=MESH
        )
        return carry

    lax.fori_loop(1, n, greet, 0)

    def splat(value):
        return jnp.full((1, 1, LANES), value, f32)

    coef, live = [], []
    for t in range(tiles):
        index = fibre_index[0, 0, t]
        fx, fy, fz = frame_of(splat(angle_s[0, index]), splat(angle_s[1, index]))
        across = splat(conduct[1, index])
        spread = splat(conduct[0, index]) - across
        alive = splat(jnp.where(active[0, 0, t] > 0, 1.0, 0.0).astype(f32))
        live.append(alive)
        coef.append(
            [
                (across + spread * fx * fx) * alive,
                (across + spread * fy * fy) * alive,
                (across + spread * fz * fz) * alive,
                spread * fx * fy * alive,
                spread * fx * fz * alive,
                spread * fy * fz * alive,
            ]
        )

    chunk = 4

    def ionic(source, t):
        alive = live[t] > 0.5

        def step(i, carry):
            at = pl.ds(t * TLX + i * chunk, chunk)
            volt = source[0, at]
            current = jnp.zeros_like(volt)
            for g in range(gates_n):
                inv = 1.0 / splat(gate_slope[g])
                keep = jnp.exp(-1.0 / splat(gate_tau[g]))
                steady = sigmoid((volt - splat(gate_half[g])) * inv)
                old = source[1 + g, at]
                gate = steady + (old - steady) * keep
                current = current + splat(conductance[g]) * gate * (volt - splat(reversal[g]))
                out[1 + g, at] = jnp.where(alive, gate, old)
            old = source[NSTATE - 1, at]
            calcium = old * calcium_keep + (1.0 - calcium_keep) * sigmoid(8.0 * (volt - 0.5))
            out[NSTATE - 1, at] = jnp.where(alive, calcium, old)
            vs[at] = jnp.where(alive, volt - current, volt)
            return carry

        lax.fori_loop(0, TLX // chunk, step, 0)

    def face_copies(stage, low_x, high_x):
        near = [(cx, mx), (cy, my), (cz, mz)]
        made = []
        for dim in range(3):
            for side in range(2):
                if dim == 0:
                    src = high_x if side == 0 else low_x
                    dst = halo_x.at[stage, side]
                elif dim == 1:
                    src, dst = send_y.at[stage, side], halo_y.at[stage, side]
                else:
                    src, dst = send_z.at[stage, side], halo_z.at[stage, side]
                at, count = near[dim]
                to = [cx, cy, cz]
                to[dim] = (at + (1 if side == 0 else count - 1)) % count
                made.append(
                    pltpu.make_async_remote_copy(
                        src_ref=src,
                        dst_ref=dst,
                        send_sem=face_send_sem.at[stage, 2 * dim + side],
                        recv_sem=face_recv_sem.at[stage, 2 * dim + side],
                        device_id=tuple(to),
                        device_id_type=MESH,
                    )
                )
        return made

    def flat_z(a):
        return jnp.transpose(a.reshape(nx * ny, nz))

    def send_faces(stage, a_y, a_z, low_x, high_x):
        send_y[stage, 0] = a_y[:, ny - 1 : ny, :]
        send_y[stage, 1] = a_y[:, 0:1, :]
        turned = flat_z(a_z)
        send_z[stage, 0] = turned[nz - 1 : nz, :]
        send_z[stage, 1] = turned[0:1, :]
        copies = face_copies(stage, low_x, high_x)
        for c in copies:
            c.start()
        return copies

    def masked(value, inside):
        return jnp.where(inside, value, 0.0)

    def diff_x(a, stage):
        low = masked(halo_x[stage, 0], cx > 0)[None]
        high = masked(halo_x[stage, 1], cx < mx - 1)[None]
        up = jnp.concatenate([a[1:], high], 0)
        down = jnp.concatenate([low, a[:-1]], 0)
        return (up - down) * 0.5

    def diff_y(a, stage):
        low = masked(halo_y[stage, 0], cy > 0)
        high = masked(halo_y[stage, 1], cy < my - 1)
        row = iota((1, ny, nz), 1)
        down = jnp.where(row == 0, low, pltpu.roll(a, 1, 1))
        up = jnp.where(row == ny - 1, high, pltpu.roll(a, ny - 1, 1))
        return (up - down) * 0.5

    def diff_z(a, stage):
        low = masked(halo_z[stage, 0], cz > 0)
        high = masked(halo_z[stage, 1], cz < mz - 1)
        row = iota((nz, nx * ny), 0)
        edge = jnp.where(row == 0, low, jnp.where(row == nz - 1, high, 0.0))
        edge = jnp.transpose(edge).reshape(nx, ny, nz)
        lane = iota((1, 1, nz), 2)
        down = jnp.where(lane == 0, edge, pltpu.roll(a, 1, 2))
        up = jnp.where(lane == nz - 1, edge, pltpu.roll(a, nz - 1, 2))
        return (up - down) * 0.5

    def make_flux(stage):
        v = vs[...]
        gx, gy, gz = diff_x(v, stage), diff_y(v, stage), diff_z(v, stage)
        for t in range(tiles):
            at = slice(t * TLX, (t + 1) * TLX)
            xx, yy, zz, xy, xz, yz = coef[t]
            a, b, c = gx[at], gy[at], gz[at]
            flux[0, at] = xx * a + xy * b + xz * c
            flux[1, at] = xy * a + yy * b + yz * c
            flux[2, at] = xz * a + yz * b + zz * c

    def finish(stage):
        lap = diff_x(flux[0], stage) + diff_y(flux[1], stage) + diff_z(flux[2], stage)
        for t in range(tiles):
            at = slice(t * TLX, (t + 1) * TLX)
            out[0, at] = vs[at] + live[t] * lap[at]

    def all_copy(k, kind, src, dst):
        return pltpu.make_async_remote_copy(
            src_ref=src.at[(me + k) % n],
            dst_ref=dst.at[me],
            send_sem=all_send_sem.at[kind, k],
            recv_sem=all_recv_sem.at[kind, k],
            device_id=coords((me + k) % n),
            device_id_type=MESH,
        )

    def all_start(kind, src, dst):
        dst[pl.ds(me, 1)] = src[pl.ds(me, 1)]

        def go(k, carry):
            all_copy(k, kind, src, dst).start()
            return carry

        lax.fori_loop(1, n, go, 0)

    def all_wait(kind, src, dst):
        def go(k, carry):
            pltpu.make_async_remote_copy(
                src_ref=src.at[(me + k) % n],
                dst_ref=dst.at[(me + n - k) % n],
                send_sem=all_send_sem.at[kind, k],
                recv_sem=all_recv_sem.at[kind, k],
                device_id=coords((me + k) % n),
                device_id_type=MESH,
            ).wait()
            return carry

        lax.fori_loop(1, n, go, 0)

    per_row = LANES // seats
    groups = slots // LANES

    def lanes_of(got):
        pieces = []
        for g in range(groups):
            pieces.append(
                lax.fori_loop(
                    0,
                    per_row,
                    lambda r, acc, g=g: acc + got[g * per_row + r],
                    jnp.zeros((1, LANES), f32),
                )
            )
        return jnp.concatenate(pieces, 1)

    for t in range(tiles):
        ionic(states, t)
    shift = elem_count.bit_length() - 1

    def flat_row(ref):
        place = lax.rem(iota((by, blocks), 1), plane)
        spread = jnp.zeros((bz, blocks), f32)
        for i in range(bx):
            put = onehot(place == iota((by, blocks), 0) + i * by)
            for part in parts3(ref[i].astype(f32)):
                spread = spread + mm(part, put)
        mine = iota((bz, blocks), 1) // plane == iota((bz, blocks), 0)
        return jnp.sum(jnp.where(mine, spread, 0.0), axis=0, keepdims=True)

    ids = flat_row(ids_ref).astype(jnp.int32)
    weight_col = column(flat_row(weight_ref))
    owner = lax.shift_right_logical(ids, shift)
    local = ids - owner * elem_count
    owner_col = column(owner.astype(f32))
    owner_f = owner.astype(f32)
    owner_cols = jnp.concatenate([owner_col] * (blocks // LANES), 1)
    earlier = (owner_cols == owner_f) & (iota((blocks, blocks), 1) < iota((blocks, blocks), 0))
    rank = jnp.sum(jnp.where(earlier, 1.0, 0.0), axis=1, keepdims=True)
    offset = ((me % per_row) * seats).astype(f32)
    rank_hit = onehot(iota((blocks, LANES), 1).astype(f32) == rank + offset)
    rank_oh[...] = rank_hit
    owned = owner == iota((n, blocks), 0)
    owner_oh[...] = onehot(owned)
    slot_col = owner_col[:, 0:1] * seats + rank
    slot_oh[...] = onehot(iota((blocks, slots), 1).astype(f32) == slot_col)
    wanted = jnp.where(owned, local.astype(f32) + 1.0, 0.0).astype(bf16)
    ids_send[...] = mm(wanted, rank_hit).reshape(n, 1, LANES)

    pl.semaphore_wait(barrier, n - 1)
    v0 = vs[...]
    stage0 = send_faces(0, v0, v0, vs.at[0], vs.at[nx - 1])
    all_start(0, ids_send, ids_got)

    nodes = pick_rows([node_disp[i : i + 1, :] for i in range(3)], (8, node_count))
    nodes3 = rows3(nodes)
    for q in range(corners):
        hit = onehot(iota((node_count, elem_count), 0) == elem_node[q : q + 1, :])
        corner_oh[q] = hit
        corner_cd[q] = fold3(mm(nodes3, hit))

    for c in stage0:
        c.wait()
    make_flux(0)
    stage1 = send_faces(1, flux[1], flux[2], flux.at[0, 0], flux.at[0, nx - 1])

    all_wait(0, ids_send, ids_got)
    asked = column(lanes_of(ids_got)) - 1.0
    asked = jnp.concatenate([asked] * (elem_count // LANES), 1)
    pick_oh[...] = onehot(iota((slots, elem_count), 1).astype(f32) == asked)
    table = jnp.concatenate(
        [corner_cd[...].reshape(corners * 8, elem_count), jnp.zeros((LANES - corners * 8, elem_count), f32)],
        0,
    )
    ans_send[...] = mm_right3(pick_oh[...], table, NT).reshape(n, seats, LANES)
    all_start(1, ans_send, ans_got)

    for c in stage1:
        c.wait()
    finish(1)
    for t in range(tiles):
        ionic(out, t)
    v1 = vs[...]
    stage2 = send_faces(2, v1, v1, vs.at[0], vs.at[nx - 1])

    calcium = out[NSTATE - 1]
    square = calcium * calcium
    pull = (square / (square + tension_half)).reshape(bx, SBX, ny, nz)
    pull = (pull[:, 0] + pull[:, 1]).reshape(bx * ny, nz)
    pair = onehot(iota((plane, bx * ny), 1) // SBY == iota((plane, bx * ny), 0))
    pooled = mm_right3(pair, pull)
    strip = onehot(iota((nz, LANES), 0) // SBZ == iota((nz, LANES), 1))
    pooled = fold3(mm(rows3(pooled), strip)) * (1.0 / (SBX * SBY * SBZ))
    worth = jnp.concatenate(
        [
            jnp.broadcast_to(pooled[:, b : b + 1], (plane, LANES))
            for b in range(bz)
        ],
        0,
    )
    worth = jnp.where(rank_oh[...].astype(f32) > 0.5, worth * weight_col, 0.0)
    val_send[...] = mm_right3(owner_oh[...], worth).reshape(n, 1, LANES)
    all_start(2, val_send, val_got)

    angle = angle_v[...]
    fx, fy, fz = frame_of(angle[0:1, :], angle[1:2, :])
    entries = angle.shape[1]
    fibres = pick_rows([fx, fy, fz], (8, entries))
    which = onehot(iota((entries, elem_count), 0) == elem_fibre[...])
    frames = fold3(mm(rows3(fibres), which))
    frame = [frames[i : i + 1, :] for i in range(3)]
    grads = [
        [((2 * (q // 4) - 1) / 4), ((2 * (q // 2 % 2) - 1) / 4), ((2 * (q % 2) - 1) / 4)]
        for q in range(corners)
    ]
    sums = [sum(corner_cd[q] * grads[q][j] for q in range(corners)) for j in range(3)]
    d = [
        [sums[j][i : i + 1, :] + (1.0 if i == j else 0.0) for j in range(3)] for i in range(3)
    ]
    cof = [
        [
            d[(i + 1) % 3][(j + 1) % 3] * d[(i + 2) % 3][(j + 2) % 3]
            - d[(i + 1) % 3][(j + 2) % 3] * d[(i + 2) % 3][(j + 1) % 3]
            for j in range(3)
        ]
        for i in range(3)
    ]
    volume = d[0][0] * cof[0][0] + d[0][1] * cof[0][1] + d[0][2] * cof[0][2]
    inverse = 1.0 / volume
    logv = jnp.log(volume)
    shear, bulk, scale = material[0], material[1], material[2]
    passive = [
        [
            shear * (d[i][j] - cof[i][j] * inverse) + bulk * logv * (cof[i][j] * inverse)
            for j in range(3)
        ]
        for i in range(3)
    ]
    stretch = [
        scale * (d[i][0] * frame[0] + d[i][1] * frame[1] + d[i][2] * frame[2]) for i in range(3)
    ]

    for c in stage2:
        c.wait()
    make_flux(2)
    stage3 = send_faces(3, flux[1], flux[2], flux.at[0, 0], flux.at[0, nx - 1])

    all_wait(1, ans_send, ans_got)
    returned = ans_got[...].reshape(slots, LANES)
    near = mm_right3(slot_oh[...], returned)
    lane = iota((plane, nz), 1)
    strip_of = lane // SBZ
    xi = ((lane % SBZ).astype(f32) + 0.5) / SBZ
    for c in range(3):
        lines = []
        for ij in range(4):
            ends = []
            for k in range(2):
                col = (2 * ij + k) * 8 + c
                value = jnp.zeros((plane, nz), f32)
                for b in range(bz):
                    value = jnp.where(
                        strip_of == b, near[b * plane : (b + 1) * plane, col : col + 1], value
                    )
                ends.append(value)
            lines.append(ends[0] * (1.0 - xi) + ends[1] * xi)
        for iv in range(SBX):
            wx = (iv + 0.5) / SBX
            for jv in range(SBY):
                wy = (jv + 0.5) / SBY
                value = (
                    lines[0] * ((1 - wx) * (1 - wy))
                    + lines[1] * ((1 - wx) * wy)
                    + lines[2] * (wx * (1 - wy))
                    + lines[3] * (wx * wy)
                )
                for p in range(bx):
                    fine_out[c, SBX * p + iv, pl.ds(jv, by, stride=SBY), :] = value[
                        p * by : (p + 1) * by
                    ]

    for c in stage3:
        c.wait()
    finish(3)

    all_wait(2, val_send, val_got)
    arrived = jnp.broadcast_to(lanes_of(val_got), (8, slots))
    tension = fold3(mm(rows3(arrived), pick_oh[...]))[0:1, :]
    total = jnp.zeros((24, node_count), f32)
    stress = [
        [passive[i][j] + tension * stretch[i] * frame[j] for j in range(3)] for i in range(3)
    ]
    for q in range(corners):
        force = pick_rows(
            [
                stress[i][0] * grads[q][0] + stress[i][1] * grads[q][1] + stress[i][2] * grads[q][2]
                for i in range(3)
            ],
            (8, elem_count),
        )
        total = total + mm(rows3(force), corner_oh[q], NT)
    resid_out[...] = fold3(total)[0:3, :]


def shards(
    states,
    active,
    fibre_index,
    fibre_angle,
    conduct,
    gate_half,
    gate_slope,
    gate_tau,
    conductance,
    reversal,
    block_elem,
    block_weight,
    node_disp,
    elem_node,
    elem_fibre,
    material,
):
    mx, my, mz = (lax.axis_size(a) for a in AXES)
    n = mx * my * mz
    elem_count = elem_node.shape[1]
    node_count = node_disp.shape[1]
    nx, ny, nz = states.shape[1:]
    bx, by, bz = block_elem.shape
    blocks = bx * by * bz
    seats = max(2 * blocks // n, 8)
    slots = n * seats
    ids = block_elem.transpose(0, 2, 1)
    weight = block_weight.transpose(0, 2, 1)
    vmem = pl.BlockSpec(memory_space=pltpu.VMEM)
    smem = pl.BlockSpec(memory_space=pltpu.SMEM)
    stages = 2 * FINE_STEPS
    return pl.pallas_call(
        functools.partial(body, (mx, my, mz, seats, elem_count)),
        out_shape=(
            jax.ShapeDtypeStruct(states.shape, f32),
            jax.ShapeDtypeStruct((3, nx, ny, nz), f32),
            jax.ShapeDtypeStruct((3, node_count), f32),
        ),
        in_specs=[vmem, smem, smem, smem, vmem] + [smem] * 6 + [vmem] * 5 + [smem],
        out_specs=(vmem, vmem, vmem),
        scratch_shapes=[
            pltpu.VMEM((nx, ny, nz), f32),
            pltpu.VMEM((3, nx, ny, nz), f32),
            pltpu.VMEM((stages, 2, nx, 1, nz), f32),
            pltpu.VMEM((stages, 2, 1, nx * ny), f32),
            pltpu.VMEM((stages, 2, ny, nz), f32),
            pltpu.VMEM((stages, 2, nx, 1, nz), f32),
            pltpu.VMEM((stages, 2, 1, nx * ny), f32),
            pltpu.VMEM((8, node_count, elem_count), bf16),
            pltpu.VMEM((8, 8, elem_count), f32),
            pltpu.VMEM((blocks, slots), bf16),
            pltpu.VMEM((slots, elem_count), bf16),
            pltpu.VMEM((n, blocks), bf16),
            pltpu.VMEM((blocks, LANES), bf16),
            pltpu.VMEM((n, 1, LANES), f32),
            pltpu.VMEM((n, 1, LANES), f32),
            pltpu.VMEM((n, 1, LANES), f32),
            pltpu.VMEM((n, 1, LANES), f32),
            pltpu.VMEM((n, seats, LANES), f32),
            pltpu.VMEM((n, seats, LANES), f32),
            pltpu.SemaphoreType.DMA((stages, 6)),
            pltpu.SemaphoreType.DMA((stages, 6)),
            pltpu.SemaphoreType.DMA((3, n)),
            pltpu.SemaphoreType.DMA((3, n)),
        ],
        compiler_params=pltpu.CompilerParams(
            collective_id=0, has_side_effects=True, vmem_limit_bytes=60 * 1024 * 1024
        ),
        name="step",
    )(
        states,
        active.transpose(1, 2, 0),
        fibre_index.transpose(1, 2, 0),
        fibre_angle,
        fibre_angle,
        conduct,
        gate_half,
        gate_slope,
        gate_tau,
        conductance,
        reversal,
        ids,
        weight,
        node_disp,
        elem_node,
        elem_fibre.reshape(1, elem_count),
        material,
    )


def solution(mesh):
    in_specs = (
        P(None, "gx", "gy", "gz"),
        P("gx", "gy", "gz"),
        P("gx", "gy", "gz"),
        P(),
        P(),
        P(),
        P(),
        P(),
        P(),
        P(),
        P("gx", "gy", "gz"),
        P("gx", "gy", "gz"),
        P(None, ("gx", "gy", "gz")),
        P(None, ("gx", "gy", "gz")),
        P(("gx", "gy", "gz")),
        P(),
    )
    out_specs = (P(None, "gx", "gy", "gz"), P(None, "gx", "gy", "gz"), P(None, ("gx", "gy", "gz")))
    return jax.shard_map(shards, mesh=mesh, in_specs=in_specs, out_specs=out_specs, check_vma=False)
```
